256 devices in a mesh: chan: 32 (over z, y), sky: 8 (over x, core).
Axes of the slice: x: 4, y: 4, z: 8, core: 2. Of those that a mesh axis runs over, the one named last changes fastest.
Arguments:
- sky_map: float32 [1024, 131072], P('chan', 'sky')
- templates: float32 [1024, 30], replicated, may hold values from -6 to 6
- noise_var: float32 [1024], replicated, may hold values from 0.5 to 2
- block_order: int32 [8, 128], P('sky'), may hold values from 0 to 127, each once within a row
- patch_count: int32 [8, 32], P('sky'), may hold values from 1 to 8, as said below
- slab_dest: int32 [8, 32, 8], P('sky'), may hold values from 0 to 7, as said below
Outputs:
- slab_cube: float32 [1024, 2048, 128], P('chan', 'sky')
The draws below stay inside these ranges and needn't reach their ends.
Inputs may be any that keep to these rules, and one draw needn't show every extreme that they name: `slab_dest`: taken in order of owners and then slots, the live slots of a sky group (slots below the owner's count) cycle through all 8 slabs in one fixed order, so every slab gets exactly 16 live slots of each group and no owner names a slab more than 1 times; slots at or beyond the owner's count are ignored. `patch_count`: in each sky group the counts sum to 128 and the largest is 8. `block_order`: each row is an ordering of the group's 128 blocks.
All inputs are finite; a program needn't handle non-finite values.
Results may differ from the reference program's by a relative error of at most 0.0003.
Values sent between devices are 32-bit elements; how exact they have to be, the bound alone decides.
A program may use at most 64 MiB of HBM per device.

```python
import math
import jax
import jax.numpy as jnp
from jax import lax

NU = 1024
NT = 30
BLK = 128
BPO = 4
CAP = 8
DCAP = 1
NB_G = 128
PIX = 131072
SLAB_ROWS = 256
N_CHAN = 32
N_SKY = 8


def draw_sky_map(key, part):
    key_chan, key_pixel, key_base, key_spectra, key_strength = jax.random.split(jax.random.fold_in(key, 11), 5)
    chan_scale = jnp.exp(jax.random.uniform(key_chan, (NU, 1), jnp.float32, math.log(0.3), math.log(3.0)))
    pixel_scale = jnp.exp(jax.random.uniform(key_pixel, (1, PIX), jnp.float32, math.log(0.1), math.log(10.0)))
    spectra = jax.random.normal(key_spectra, (NU, 6), jnp.float32)
    strengths = jax.random.normal(key_strength, (6, PIX), jnp.float32)
    field_sum = jax.random.normal(key_base, (NU, PIX), jnp.float32)
    gain_low = 0.3
    gain_high = 1.2
    for mode_index in range(6):
        gain_value = gain_low * (gain_high / gain_low) ** (mode_index / 5.0)
        field_sum = field_sum + gain_value * spectra[:, mode_index:mode_index + 1] * strengths[mode_index:mode_index + 1, :]
    return (field_sum * chan_scale * pixel_scale).astype(jnp.float32)


def group_counts(group_key):
    key_perm, key_pair = jax.random.split(group_key, 2)
    order = jax.random.permutation(key_perm, N_CHAN)
    rank = jnp.arange(N_CHAN, dtype=jnp.int32)
    pair_index = jnp.maximum(rank - 3, 0) // 2
    sign_value = jnp.where((rank - 3) % 2 == 0, 1, -1)
    has_partner = (rank >= 3) & (pair_index * 2 + 4 < N_CHAN)
    shifts = jax.random.randint(key_pair, (N_CHAN,), -(BPO - 1), BPO)
    by_rank = BPO + jnp.where(has_partner, sign_value * jnp.take(shifts, pair_index), 0)
    by_rank = jnp.where(rank == 0, CAP, by_rank)
    by_rank = jnp.where(rank == 1, 1, by_rank)
    by_rank = jnp.where(rank == 2, BPO - 1, by_rank)
    return jnp.zeros((N_CHAN,), jnp.int32).at[order].set(by_rank.astype(jnp.int32))


def shared_counts(key):
    group_keys = jax.random.split(jax.random.fold_in(key, 31), N_SKY)
    return jax.vmap(group_counts)(group_keys).astype(jnp.int32)


def draw_patch_count(key, part):
    return shared_counts(key)


def draw_slab_dest(key, part):
    counts = shared_counts(key)
    group_keys = jax.random.split(jax.random.fold_in(key, 37), N_SKY)

    def one_group(group_key, counts_row):
        key_shift, key_label = jax.random.split(group_key, 2)
        shift = jax.random.randint(key_shift, (), 0, N_SKY)
        labels = jax.random.permutation(key_label, N_SKY).astype(jnp.int32)
        offsets = jnp.cumsum(counts_row) - counts_row
        slot_index = jnp.arange(CAP, dtype=jnp.int32)
        position = offsets[:, None] + slot_index[None, :]
        live = jnp.take(labels, (position + shift) % N_SKY)
        return jnp.where(slot_index[None, :] < counts_row[:, None], live, slot_index[None, :] % N_SKY)
    return jax.vmap(one_group)(group_keys, counts).astype(jnp.int32)


def bell_draw(own_key, extent, width, reach, held_as=jnp.bfloat16):
    array = width * jax.random.normal(own_key, extent, jnp.float32)
    return jnp.clip(array, min=-reach, max=reach).astype(held_as)


def setup_inputs(seed: int = 0) -> dict:
    key_of = jax.random.split(jax.random.key(seed), 7)
    return {
        "sky_map": draw_sky_map(jax.random.fold_in(key_of[6], 71), 0),
        "templates": bell_draw(key_of[1], (NU, NT), 1.0, 6.0, jnp.float32),
        "noise_var": jnp.clip(jnp.exp(jax.random.uniform(key_of[2], (NU,), jnp.float32, math.log(0.5), math.log(2.0))), 0.5, 2.0),
        "block_order": jax.vmap(lambda own: jax.random.permutation(own, NB_G))(jax.random.split(key_of[3], N_SKY)).reshape((N_SKY, NB_G)).astype(jnp.int32),
        "patch_count": draw_patch_count(jax.random.fold_in(key_of[6], 71), 0),
        "slab_dest": draw_slab_dest(jax.random.fold_in(key_of[6], 71), 0),
    }


def owner_blocks(order_row, counts_row):
    offsets = jnp.cumsum(counts_row) - counts_row
    slot_index = jnp.arange(CAP, dtype=jnp.int32)
    live_slots = slot_index[None, :] < counts_row[:, None]
    position = jnp.where(live_slots, offsets[:, None] + slot_index[None, :], 0).astype(jnp.int32)
    return (jnp.take(order_row, position, axis=0), live_slots)

def slab_sources(dest_row, block_count, sky_count, slab_cap):
    slot_index = jnp.arange(dest_row.shape[0], dtype=jnp.int32)
    live_slots = slot_index < block_count
    earlier = (dest_row[:, None] == dest_row[None, :]) & live_slots[:, None] & live_slots[None, :] & (slot_index[None, :] < slot_index[:, None])
    rank_in_slab = jnp.sum(earlier.astype(jnp.int32), axis=1)
    target_row = dest_row * slab_cap + rank_in_slab
    row_index = jnp.arange(sky_count * slab_cap, dtype=jnp.int32)
    matches = (target_row[None, :] == row_index[:, None]) & live_slots[None, :]
    source_slot = jnp.sum(jnp.where(matches, slot_index[None, :], 0), axis=1).astype(jnp.int32)
    return (source_slot, jnp.any(matches, axis=1))

def template_amplitudes(pixels, block_count, templates, noise_var):
    highest = lax.Precision.HIGHEST
    covariance = jnp.dot(pixels, pixels.T, precision=highest) / (block_count * BLK).astype(jnp.float32) + jnp.diag(noise_var)
    factor = jnp.linalg.cholesky(covariance)
    weighted = jax.scipy.linalg.cho_solve((factor, True), templates)
    gram_matrix = jnp.dot(templates.T, weighted, precision=highest)
    projected = jnp.dot(weighted.T, pixels, precision=highest)
    return jax.scipy.linalg.cho_solve((jnp.linalg.cholesky(gram_matrix), True), projected)

def reference(sky_map, templates, noise_var, block_order, patch_count, slab_dest):
    group_cube = sky_map.reshape(NU, N_SKY, NB_G, BLK)

    def one_owner(owner_index):
        group_index = owner_index // N_CHAN
        member = owner_index % N_CHAN
        blocks, live_slots = owner_blocks(block_order[group_index], patch_count[group_index])
        own_blocks = blocks[member]
        own_live = live_slots[member]
        block_count = patch_count[group_index, member]
        group_part = lax.dynamic_index_in_dim(group_cube, group_index, 1, keepdims=False)
        pixels = jnp.take(group_part, own_blocks, axis=1)
        pixels = jnp.where(own_live[None, :, None], pixels, 0.0).reshape(NU, CAP * BLK)
        amplitudes = template_amplitudes(pixels, block_count, templates, noise_var)
        cleaned = pixels - jnp.dot(templates, amplitudes, precision=lax.Precision.HIGHEST)
        source_slot, filled = slab_sources(slab_dest[group_index, member], block_count, N_SKY, DCAP)
        slab_block = jnp.take(cleaned.reshape(NU, CAP, BLK), source_slot, axis=1)
        return jnp.where(filled[None, :, None], slab_block, 0.0)
    owners = lax.map(one_owner, jnp.arange(N_SKY * N_CHAN, dtype=jnp.int32))
    owners = owners.reshape(N_SKY, N_CHAN, NU, N_SKY, DCAP, BLK)
    return jnp.transpose(owners, (2, 3, 0, 1, 4, 5)).reshape(NU, N_SKY * SLAB_ROWS, BLK)
```

```python
import functools
import jax, jax.numpy as jnp
from jax import lax
from jax.sharding import PartitionSpec as P
from jax.experimental import pallas as pl
from jax.experimental.pallas import tpu as pltpu
NU = 1024
BLK = 128
CAP = 8
HI = lax.Precision.HIGHEST
NT_DIMS = (((1,), (1,)), ((), ()))
NN_DIMS = (((1,), (0,)), ((), ()))

def mm_nn(a, b):
    return lax.dot_general(a, b, NN_DIMS, precision=HI, preferred_element_type=jnp.float32)

def invert_spd(ref, slabs):
    lane = lax.broadcasted_iota(jnp.int32, (8, 128), 1)
    sub = lax.broadcasted_iota(jnp.int32, (8, 128), 0)
    for t in range(slabs):
        lo = 8 * t
        in_slab = (lane >= lo) & (lane < lo + 8)
        rows = [jnp.broadcast_to(ref[lo + i:lo + i + 1, :], (8, 128)) for i in range(8)]
        a = {}
        for i in range(8):
            for j in range(i + 1):
                a[i, j] = jnp.broadcast_to(rows[i][:, lo + j:lo + j + 1], (8, 128))
        low, inv = {}, []
        for j in range(8):
            r = 1.0 / a[j, j]
            inv.append(r)
            for i in range(j + 1, 8):
                low[i, j] = a[i, j] * r
            for i in range(j + 1, 8):
                for m in range(j + 1, i + 1):
                    a[i, m] = a[i, m] - low[i, j] * a[m, j]
        y = []
        for i in range(8):
            v = jnp.where(in_slab, jnp.where(lane == lo + i, 1.0, 0.0), rows[i])
            for j in range(i):
                v = v - low[i, j] * y[j]
            y.append(v)
        u = [None] * 8
        for i in reversed(range(8)):
            v = y[i] * inv[i]
            for j in range(7, i, -1):
                v = v - low[j, i] * u[j]
            u[i] = v
        for g in list(range(t + 1, slabs)) + list(range(t)):
            row = ref[8 * g:8 * g + 8, :]
            acc = jnp.where(in_slab, 0.0, row)
            for j in range(8):
                acc = acc - jnp.broadcast_to(row[:, lo + j:lo + j + 1], (8, 128)) * u[j]
            ref[8 * g:8 * g + 8, :] = acc
        own = u[0]
        for i in range(1, 8):
            own = jnp.where(sub == i, u[i], own)
        ref[lo:lo + 8, :] = own

def split3(a):
    hi = a.astype(jnp.bfloat16)
    rest = a - hi.astype(jnp.float32)
    mid = rest.astype(jnp.bfloat16)
    low = (rest - mid.astype(jnp.float32)).astype(jnp.bfloat16)
    return hi, mid, low

def cat(parts):
    return jnp.concatenate(parts, axis=1)

def dot6(a, b, dims):
    def one(x, y):
        return lax.dot_general(x, y, dims, preferred_element_type=jnp.float32)
    if dims is NT_DIMS:
        return one(cat(a[:1]), b[2]) + one(cat(a[:2]), cat([b[1]] * 2)) + one(cat(a), cat([b[0]] * 3))
    up = lambda y, k: jnp.concatenate([y] * k, axis=0)
    return one(cat(a[:1]), b[2]) + one(cat(a[:2]), up(b[1], 2)) + one(cat(a), up(b[0], 3))

def gls_kernel(cnt_ref, x_ref, tt_ref, noise_ref, out_ref, xs_ref, q_ref, v_ref, p_ref, d_ref, w_ref, m_ref, nb=8):
    scale = 1.0 / (cnt_ref[0, 0] * 128).astype(jnp.float32)
    n = 128 * nb
    ext = n + 32
    row = lax.broadcasted_iota(jnp.int32, (128, 128), 0)
    col = lax.broadcasted_iota(jnp.int32, (128, 128), 1)

    def split_rows(r, carry):
        at = pl.ds(pl.multiple_of(r * 128, 128), 128)
        for i, part in enumerate(split3(x_ref[at, :])):
            xs_ref[i, at, :] = part
        return carry
    lax.fori_loop(0, nb, split_rows, 0)

    def factor(k):
        lo, hi = 128 * k, 128 * k + 128
        value = dot6(split3(p_ref[hi:ext, :]), split3(d_ref[...]), NN_DIMS)
        for i, part in enumerate(split3(value)):
            v_ref[i, hi:ext, lo:hi] = part

    def step(k, carry):
        for kk in range(nb):
            @pl.when(k == kk)
            def _(kk=kk):
                lo, hi = 128 * kk, 128 * kk + 128
                if kk:
                    factor(kk - 1)
                p_ref[n:ext, :] = tt_ref[:, lo:hi]
                p_ref[lo:n, :] = dot6([xs_ref[i, lo:n, :] for i in range(3)],
                                      [xs_ref[i, lo:hi, :] for i in range(3)], NT_DIMS) * scale
                if kk:
                    p_ref[lo:ext, :] -= dot6([v_ref[i, lo:ext, 0:lo] for i in range(3)],
                                             [q_ref[i, lo:hi, 0:lo] for i in range(3)], NT_DIMS)
                if hi < n:
                    for i, part in enumerate(split3(p_ref[hi:n, :])):
                        q_ref[i, hi:n, lo:hi] = part
                noise = jnp.broadcast_to(noise_ref[0:1, lo:hi], (128, 128))
                d_ref[...] = p_ref[lo:hi, :] + jnp.where(row == col, noise, 0.0)
        invert_spd(d_ref, 16)
        return carry
    lax.fori_loop(0, nb, step, 0)
    factor(nb - 1)
    for k in reversed(range(nb)):
        lo, hi = 128 * k, 128 * k + 128
        wk = sum(v_ref[i, n:ext, lo:hi].astype(jnp.float32) for i in (2, 1, 0))
        if hi < n:
            wk = wk - dot6([w_ref[i, :, hi:n] for i in range(3)],
                           [v_ref[i, hi:n, lo:hi] for i in range(3)], NN_DIMS)
        for i, part in enumerate(split3(wk)):
            w_ref[i, :, lo:hi] = part
    w = [w_ref[i] for i in range(3)]
    proj = dot6(w, [xs_ref[i] for i in range(3)], NN_DIMS)
    gram = dot6(w, split3(tt_pad(tt_ref, n)), NT_DIMS)
    prow = lax.broadcasted_iota(jnp.int32, (32, 128), 0)
    pcol = lax.broadcasted_iota(jnp.int32, (32, 128), 1)
    m_ref[...] = gram + jnp.where((prow == pcol) & (prow >= 30), 1.0, 0.0)
    invert_spd(m_ref, 4)
    out_ref[...] = mm_nn(m_ref[...][:, 0:32], proj)

def tt_pad(tt_ref, n):
    return jnp.concatenate([tt_ref[...], jnp.zeros((96, n), jnp.float32)], axis=0)

def gls(cnt, x, tt, noise):
    n = x.shape[0]
    nb = n // 128
    return pl.pallas_call(
        functools.partial(gls_kernel, nb=nb),
        out_shape=jax.ShapeDtypeStruct((32, x.shape[1]), jnp.float32),
        in_specs=[pl.BlockSpec(memory_space=pltpu.SMEM)] + [pl.BlockSpec(memory_space=pltpu.VMEM)] * 3,
        out_specs=pl.BlockSpec(memory_space=pltpu.VMEM),
        scratch_shapes=[pltpu.VMEM((3, n, n), jnp.bfloat16), pltpu.VMEM((3, n, n), jnp.bfloat16),
                        pltpu.VMEM((3, n + 32, n), jnp.bfloat16), pltpu.VMEM((n + 32, 128), jnp.float32),
                        pltpu.VMEM((128, 128), jnp.float32), pltpu.VMEM((3, 32, n), jnp.bfloat16),
                        pltpu.VMEM((32, 128), jnp.float32)],
        cost_estimate=pl.CostEstimate(flops=60 * 10**9, bytes_accessed=1 << 22, transcendentals=0),
        compiler_params=pltpu.CompilerParams(vmem_limit_bytes=40 << 20),
    )(cnt, x, tt, noise)


def pack_kernel(slot_ref, slab_ref, map_ref, out_ref, sky_ref):
    def put(c, carry):
        for j in range(CAP):
            block = slot_ref[c, j]
            at = pl.multiple_of(jnp.maximum(block, 0) * BLK, BLK)
            tile = map_ref[:, pl.ds(at, BLK)]
            out_ref[c, :, j * BLK:(j + 1) * BLK] = jnp.where(block >= 0, tile, 0.0)
        place = pl.multiple_of(c * BLK, BLK)
        for d in range(sky_ref.shape[0]):
            block = slab_ref[d, c]
            at = pl.multiple_of(jnp.maximum(block, 0) * BLK, BLK)
            tile = map_ref[:, pl.ds(at, BLK)]
            sky_ref[d, :, pl.ds(place, BLK)] = jnp.where(block >= 0, tile, 0.0)
        return carry
    lax.fori_loop(0, slot_ref.shape[0], put, 0)


def pack(slot_block, slab_block, sky_map):
    owners, rows = slot_block.shape[0], sky_map.shape[0]
    slabs = slab_block.shape[0]
    return pl.pallas_call(
        pack_kernel,
        out_shape=(jax.ShapeDtypeStruct((owners, rows, CAP * BLK), jnp.float32),
                   jax.ShapeDtypeStruct((slabs, rows, owners * BLK), jnp.float32)),
        in_specs=[pl.BlockSpec(memory_space=pltpu.SMEM)] * 2 + [pl.BlockSpec(memory_space=pltpu.VMEM)],
        out_specs=(pl.BlockSpec(memory_space=pltpu.VMEM),) * 2,
        compiler_params=pltpu.CompilerParams(vmem_limit_bytes=40 << 20),
    )(slot_block, slab_block, sky_map)


RINGS = (8, 4)
SPLIT = 5


def gather_plan(cost):
    time, free, queue, serial = 0.0, {}, [], 0
    events = []

    def send(now, part, axis, off, sign, hop):
        nonlocal serial
        half = hop == RINGS[axis] // 2
        groups = SPLIT if part == 0 else 8 - SPLIT
        link = (axis, sign)
        start = max(now, free.get(link, 0.0))
        free[link] = start + cost * groups * (0.5 if half else 1.0)
        serial += 1
        queue.append((free[link] + 2.0, serial, (part, axis, off, sign, hop)))
        return part, axis, off, sign, hop

    def both(now, part, axis, off):
        return [send(now, part, axis, off, sign, 1) for sign in (1, -1)]

    first = []
    for part in (0, 1):
        first += both(0.0, part, part, (0, 0))
    for part in (0, 1):
        first += both(0.0, part, 1 - part, (0, 0))
    halves = set()
    while queue:
        queue.sort()
        time, _, (part, axis, off, sign, hop) = queue.pop(0)
        moved = list(off)
        moved[axis] -= sign
        moved = tuple(moved)
        half = hop == RINGS[axis] // 2
        out = []
        if not half:
            out.append(send(time, part, axis, moved, sign, hop + 1))
        if axis == part:
            place = (part, moved[axis] % RINGS[axis])
            if not half or place in halves:
                out += both(time, part, 1 - axis, moved)
            halves.add(place)
        events.append(((part, axis, off, sign, hop), moved, out))
    return first, events, time


def gather_kernel(amp_ref, out_ref, local_sem, send_sem, recv_sem):
    chan = lax.axis_index("chan")
    place = (chan // RINGS[1], lax.rem(chan, RINGS[1]))

    def member(off):
        at = [lax.rem(place[i] + off[i] % RINGS[i], RINGS[i]) for i in (0, 1)]
        return at[0] * RINGS[1] + at[1]

    first, events, _ = gather_plan(1.0)
    number = {event[0]: k for k, event in enumerate(events)}

    def copy(key, off):
        part, axis, start, sign, hop = key
        half = hop == RINGS[axis] // 2
        groups = slice(0, SPLIT) if part == 0 else slice(SPLIT, 8)
        rows = slice(0, 32)
        if half:
            rows = slice(0, 16) if sign > 0 else slice(16, 32)
        k = number[key]
        chunk = member(off)
        step = [0, 0]
        step[axis] = sign
        own = off == (0, 0)
        src = amp_ref.at[groups, rows] if own else out_ref.at[chunk, groups, rows]
        return pltpu.make_async_remote_copy(
            src_ref=src, dst_ref=out_ref.at[chunk, groups, rows], send_sem=send_sem.at[k], recv_sem=recv_sem.at[k],
            device_id={"chan": member(step)}, device_id_type=pl.DeviceIdType.MESH)

    barrier = pltpu.get_barrier_semaphore()
    for step in ((1, 0), (-1, 0), (0, 1), (0, -1)):
        pl.semaphore_signal(barrier, inc=1, device_id={"chan": member(step)},
                            device_id_type=pl.DeviceIdType.MESH)
    pl.semaphore_wait(barrier, 4)
    sent = [copy(key, key[2]) for key in first]
    for c in sent:
        c.start()
    local = pltpu.make_async_copy(amp_ref, out_ref.at[chan], local_sem)
    local.start()
    for key, moved, out in events:
        copy(key, moved).wait_recv()
        for nxt in out:
            c = copy(nxt, nxt[2])
            c.start()
            sent.append(c)
    local.wait()
    for c in sent:
        c.wait_send()


def gather(amp):
    count = len(gather_plan(1.0)[1])
    return pl.pallas_call(
        gather_kernel,
        out_shape=jax.ShapeDtypeStruct((RINGS[0] * RINGS[1],) + amp.shape, jnp.float32),
        in_specs=[pl.BlockSpec(memory_space=pltpu.VMEM)],
        out_specs=pl.BlockSpec(memory_space=pltpu.VMEM),
        scratch_shapes=[pltpu.SemaphoreType.DMA, pltpu.SemaphoreType.DMA((count,)), pltpu.SemaphoreType.DMA((count,))],
        compiler_params=pltpu.CompilerParams(collective_id=0, has_side_effects=True, vmem_limit_bytes=40 << 20),
    )(amp)


def clean_kernel(tmpl_ref, amp_ref, raw_ref, out_ref):
    owners = amp_ref.shape[0]
    for c in range(0, owners, 8):
        amp = jnp.concatenate([amp_ref[c + i, 0] for i in range(8)], axis=1)
        rest = raw_ref[0, :, c * BLK:(c + 8) * BLK] - mm_nn(tmpl_ref[...], amp)
        for i in range(8):
            out_ref[:, c + i, :] = rest[:, i * BLK:(i + 1) * BLK]


def clean(tmpl, amp, raw):
    owners, groups = amp.shape[0], amp.shape[1]
    rows = raw.shape[1]
    return pl.pallas_call(
        clean_kernel,
        grid=(groups,),
        out_shape=jax.ShapeDtypeStruct((rows, groups * owners, BLK), jnp.float32),
        in_specs=[pl.BlockSpec(tmpl.shape, lambda g: (0, 0)),
                  pl.BlockSpec((owners, 1, amp.shape[2], BLK), lambda g: (0, g, 0, 0)),
                  pl.BlockSpec((1, rows, owners * BLK), lambda g: (g, 0, 0))],
        out_specs=pl.BlockSpec((rows, owners, BLK), lambda g: (0, g, 0)),
    )(tmpl, amp, raw)


def tables(order_row, counts_row, dest_rows, slabs):
    slot_index = jnp.arange(CAP, dtype=jnp.int32)
    offsets = jnp.cumsum(counts_row) - counts_row
    live = slot_index[None, :] < counts_row[:, None]
    position = jnp.where(live, offsets[:, None] + slot_index[None, :], 0)
    slot_block = jnp.where(live, jnp.take(order_row, position, axis=0), -1)
    bound = dest_rows[None, :, :] == jnp.arange(slabs, dtype=jnp.int32)[:, None, None]
    slab_block = jnp.max(jnp.where(bound, slot_block[None, :, :], -1), axis=2)
    return slot_block.astype(jnp.int32), slab_block.astype(jnp.int32)


def on_device(sky_map, templates, noise_var, block_order, patch_count, slab_dest):
    slabs = lax.axis_size("sky")
    member = lax.axis_index("chan")
    rows = sky_map.shape[0]
    slot_block, slab_block = tables(block_order[0], patch_count[0], slab_dest[0], slabs)
    outgoing, sky_out = pack(slot_block, slab_block, sky_map)
    pixels = lax.all_to_all(outgoing, "chan", split_axis=0, concat_axis=0, tiled=True)
    pixels = pixels.reshape(NU, CAP * BLK)
    pixels, sky_out = lax.optimization_barrier((pixels, sky_out))
    raw = lax.all_to_all(sky_out, "sky", split_axis=0, concat_axis=0, tiled=True)
    block_count = lax.dynamic_index_in_dim(patch_count[0], member, 0, keepdims=False)
    padded = jnp.pad(templates, ((0, 0), (0, 32 - templates.shape[1])))
    amp = gls(block_count.reshape(1, 1), pixels, padded.T, noise_var[None, :])
    amp, raw = lax.optimization_barrier((amp, raw))
    own_dest = lax.dynamic_index_in_dim(slab_dest[0], member, 0, keepdims=False)
    slot_index = jnp.arange(CAP, dtype=jnp.int32)
    match = (own_dest[None, :] == jnp.arange(slabs, dtype=jnp.int32)[:, None]) & (slot_index[None, :] < block_count)
    source = jnp.sum(jnp.where(match, slot_index[None, :], 0), axis=1)
    amp = jnp.take(amp.reshape(32, CAP, BLK).transpose(1, 0, 2), source, axis=0)
    amp = jnp.where(jnp.any(match, axis=1)[:, None, None], amp, 0.0)
    amp = lax.all_to_all(amp, "sky", split_axis=0, concat_axis=0, tiled=True)
    amp = gather(amp)
    own = lax.dynamic_slice_in_dim(padded, member * rows, rows, 0)
    return clean(own, amp, raw)


def solution(mesh):
    return jax.shard_map(
        on_device,
        mesh=mesh,
        in_specs=(P("chan", "sky"), P(), P(), P("sky", None), P("sky", None), P("sky", None, None)),
        out_specs=P("chan", "sky", None),
        check_vma=False,
    )
```

```python
import functools
import jax, jax.numpy as jnp
from jax import lax
from jax.sharding import PartitionSpec as P
from jax.experimental import pallas as pl
from jax.experimental.pallas import tpu as pltpu
NU = 1024
BLK = 128
CAP = 8
HI = lax.Precision.HIGHEST
NT_DIMS = (((1,), (1,)), ((), ()))
NN_DIMS = (((1,), (0,)), ((), ()))

def mm_nn(a, b):
    return lax.dot_general(a, b, NN_DIMS, precision=HI, preferred_element_type=jnp.float32)

def invert_spd(ref, slabs):
    lane = lax.broadcasted_iota(jnp.int32, (8, 128), 1)
    sub = lax.broadcasted_iota(jnp.int32, (8, 128), 0)
    for t in range(slabs):
        lo = 8 * t
        in_slab = (lane >= lo) & (lane < lo + 8)
        rows = [jnp.broadcast_to(ref[lo + i:lo + i + 1, :], (8, 128)) for i in range(8)]
        a = {}
        for i in range(8):
            for j in range(i + 1):
                a[i, j] = jnp.broadcast_to(rows[i][:, lo + j:lo + j + 1], (8, 128))
        low, inv = {}, []
        for j in range(8):
            r = 1.0 / a[j, j]
            inv.append(r)
            for i in range(j + 1, 8):
                low[i, j] = a[i, j] * r
            for i in range(j + 1, 8):
                for m in range(j + 1, i + 1):
                    a[i, m] = a[i, m] - low[i, j] * a[m, j]
        y = []
        for i in range(8):
            v = jnp.where(in_slab, jnp.where(lane == lo + i, 1.0, 0.0), rows[i])
            for j in range(i):
                v = v - low[i, j] * y[j]
            y.append(v)
        u = [None] * 8
        for i in reversed(range(8)):
            v = y[i] * inv[i]
            for j in range(7, i, -1):
                v = v - low[j, i] * u[j]
            u[i] = v
        for g in list(range(t + 1, slabs)) + list(range(t)):
            row = ref[8 * g:8 * g + 8, :]
            acc = jnp.where(in_slab, 0.0, row)
            for j in range(8):
                acc = acc - jnp.broadcast_to(row[:, lo + j:lo + j + 1], (8, 128)) * u[j]
            ref[8 * g:8 * g + 8, :] = acc
        own = u[0]
        for i in range(1, 8):
            own = jnp.where(sub == i, u[i], own)
        ref[lo:lo + 8, :] = own

def split3(a):
    hi = a.astype(jnp.bfloat16)
    rest = a - hi.astype(jnp.float32)
    mid = rest.astype(jnp.bfloat16)
    low = (rest - mid.astype(jnp.float32)).astype(jnp.bfloat16)
    return hi, mid, low

def cat(parts):
    return jnp.concatenate(parts, axis=1)

def dot6(a, b, dims):
    def one(x, y):
        return lax.dot_general(x, y, dims, preferred_element_type=jnp.float32)
    if dims is NT_DIMS:
        return one(cat(a[:1]), b[2]) + one(cat(a[:2]), cat([b[1]] * 2)) + one(cat(a), cat([b[0]] * 3))
    up = lambda y, k: jnp.concatenate([y] * k, axis=0)
    return one(cat(a[:1]), b[2]) + one(cat(a[:2]), up(b[1], 2)) + one(cat(a), up(b[0], 3))

def gls_kernel(cnt_ref, x_ref, tt_ref, noise_ref, out_ref, xs_ref, q_ref, v_ref, p_ref, d_ref, w_ref, m_ref, nb=8):
    scale = 1.0 / (cnt_ref[0, 0] * 128).astype(jnp.float32)
    n = 128 * nb
    ext = n + 32
    row = lax.broadcasted_iota(jnp.int32, (128, 128), 0)
    col = lax.broadcasted_iota(jnp.int32, (128, 128), 1)

    def split_rows(r, carry):
        at = pl.ds(pl.multiple_of(r * 128, 128), 128)
        for i, part in enumerate(split3(x_ref[at, :])):
            xs_ref[i, at, :] = part
        return carry
    lax.fori_loop(0, nb, split_rows, 0)

    def factor(k):
        lo, hi = 128 * k, 128 * k + 128
        value = dot6(split3(p_ref[hi:ext, :]), split3(d_ref[...]), NN_DIMS)
        for i, part in enumerate(split3(value)):
            v_ref[i, hi:ext, lo:hi] = part

    def step(k, carry):
        for kk in range(nb):
            @pl.when(k == kk)
            def _(kk=kk):
                lo, hi = 128 * kk, 128 * kk + 128
                if kk:
                    factor(kk - 1)
                p_ref[n:ext, :] = tt_ref[:, lo:hi]
                p_ref[lo:n, :] = dot6([xs_ref[i, lo:n, :] for i in range(3)],
                                      [xs_ref[i, lo:hi, :] for i in range(3)], NT_DIMS) * scale
                if kk:
                    p_ref[lo:ext, :] -= dot6([v_ref[i, lo:ext, 0:lo] for i in range(3)],
                                             [q_ref[i, lo:hi, 0:lo] for i in range(3)], NT_DIMS)
                if hi < n:
                    for i, part in enumerate(split3(p_ref[hi:n, :])):
                        q_ref[i, hi:n, lo:hi] = part
                noise = jnp.broadcast_to(noise_ref[0:1, lo:hi], (128, 128))
                d_ref[...] = p_ref[lo:hi, :] + jnp.where(row == col, noise, 0.0)
        invert_spd(d_ref, 16)
        return carry
    lax.fori_loop(0, nb, step, 0)
    factor(nb - 1)
    for k in reversed(range(nb)):
        lo, hi = 128 * k, 128 * k + 128
        wk = sum(v_ref[i, n:ext, lo:hi].astype(jnp.float32) for i in (2, 1, 0))
        if hi < n:
            wk = wk - dot6([w_ref[i, :, hi:n] for i in range(3)],
                           [v_ref[i, hi:n, lo:hi] for i in range(3)], NN_DIMS)
        for i, part in enumerate(split3(wk)):
            w_ref[i, :, lo:hi] = part
    w = [w_ref[i] for i in range(3)]
    proj = dot6(w, [xs_ref[i] for i in range(3)], NN_DIMS)
    gram = dot6(w, split3(tt_pad(tt_ref, n)), NT_DIMS)
    prow = lax.broadcasted_iota(jnp.int32, (32, 128), 0)
    pcol = lax.broadcasted_iota(jnp.int32, (32, 128), 1)
    m_ref[...] = gram + jnp.where((prow == pcol) & (prow >= 30), 1.0, 0.0)
    invert_spd(m_ref, 4)
    out_ref[...] = mm_nn(m_ref[...][:, 0:32], proj)

def tt_pad(tt_ref, n):
    return jnp.concatenate([tt_ref[...], jnp.zeros((96, n), jnp.float32)], axis=0)

def gls(cnt, x, tt, noise):
    n = x.shape[0]
    nb = n // 128
    return pl.pallas_call(
        functools.partial(gls_kernel, nb=nb),
        out_shape=jax.ShapeDtypeStruct((32, x.shape[1]), jnp.float32),
        in_specs=[pl.BlockSpec(memory_space=pltpu.SMEM)] + [pl.BlockSpec(memory_space=pltpu.VMEM)] * 3,
        out_specs=pl.BlockSpec(memory_space=pltpu.VMEM),
        scratch_shapes=[pltpu.VMEM((3, n, n), jnp.bfloat16), pltpu.VMEM((3, n, n), jnp.bfloat16),
                        pltpu.VMEM((3, n + 32, n), jnp.bfloat16), pltpu.VMEM((n + 32, 128), jnp.float32),
                        pltpu.VMEM((128, 128), jnp.float32), pltpu.VMEM((3, 32, n), jnp.bfloat16),
                        pltpu.VMEM((32, 128), jnp.float32)],
        cost_estimate=pl.CostEstimate(flops=60 * 10**9, bytes_accessed=1 << 22, transcendentals=0),
        compiler_params=pltpu.CompilerParams(vmem_limit_bytes=40 << 20),
    )(cnt, x, tt, noise)


def slot_kernel(slot_ref, map_ref, out_ref):
    def put(c, carry):
        for j in range(CAP):
            block = slot_ref[c, j]
            at = pl.multiple_of(jnp.maximum(block, 0) * BLK, BLK)
            tile = map_ref[:, pl.ds(at, BLK)]
            out_ref[c, :, j * BLK:(j + 1) * BLK] = jnp.where(block >= 0, tile, 0.0)
        return carry
    lax.fori_loop(0, slot_ref.shape[0], put, 0)


def slab_kernel(slab_ref, map_ref, out_ref):
    def put(c, carry):
        place = pl.multiple_of(c * BLK, BLK)
        for d in range(out_ref.shape[0]):
            block = slab_ref[d, c]
            at = pl.multiple_of(jnp.maximum(block, 0) * BLK, BLK)
            tile = map_ref[:, pl.ds(at, BLK)]
            out_ref[d, :, pl.ds(place, BLK)] = jnp.where(block >= 0, tile, 0.0)
        return carry
    lax.fori_loop(0, slab_ref.shape[1], put, 0)


def pack(kernel, blocks, shape, sky_map):
    return pl.pallas_call(
        kernel,
        out_shape=jax.ShapeDtypeStruct(shape, jnp.float32),
        in_specs=[pl.BlockSpec(memory_space=pltpu.SMEM), pl.BlockSpec(memory_space=pltpu.VMEM)],
        out_specs=pl.BlockSpec(memory_space=pltpu.VMEM),
        cost_estimate=pl.CostEstimate(flops=10**6, bytes_accessed=6 << 20, transcendentals=0),
        compiler_params=pltpu.CompilerParams(vmem_limit_bytes=40 << 20),
    )(blocks, sky_map)


RINGS = (8, 4)
SPLIT = 5


def gather_plan(cost):
    time, free, queue, serial = 0.0, {}, [], 0
    events = []

    def send(now, part, axis, off, sign, hop):
        nonlocal serial
        half = hop == RINGS[axis] // 2
        groups = SPLIT if part == 0 else 8 - SPLIT
        link = (axis, sign)
        start = max(now, free.get(link, 0.0))
        free[link] = start + cost * groups * (0.5 if half else 1.0)
        serial += 1
        queue.append((free[link] + 2.0, serial, (part, axis, off, sign, hop)))
        return part, axis, off, sign, hop

    def both(now, part, axis, off):
        return [send(now, part, axis, off, sign, 1) for sign in (1, -1)]

    first = []
    for part in (0, 1):
        first += both(0.0, part, part, (0, 0))
    for part in (0, 1):
        first += both(0.0, part, 1 - part, (0, 0))
    halves = set()
    while queue:
        queue.sort()
        time, _, (part, axis, off, sign, hop) = queue.pop(0)
        moved = list(off)
        moved[axis] -= sign
        moved = tuple(moved)
        half = hop == RINGS[axis] // 2
        out = []
        if not half:
            out.append(send(time, part, axis, moved, sign, hop + 1))
        if axis == part:
            place = (part, moved[axis] % RINGS[axis])
            if not half or place in halves:
                out += both(time, part, 1 - axis, moved)
            halves.add(place)
        events.append(((part, axis, off, sign, hop), moved, out))
    return first, events, time


def gather_kernel(amp_ref, out_ref, own_ref, local_sem, send_sem, recv_sem, sky_send_sem, sky_recv_sem):
    chan = lax.axis_index("chan")
    sky = lax.axis_index("sky")
    slabs = amp_ref.shape[0]
    place = (chan // RINGS[1], lax.rem(chan, RINGS[1]))

    def member(off):
        at = [lax.rem(place[i] + off[i] % RINGS[i], RINGS[i]) for i in (0, 1)]
        return at[0] * RINGS[1] + at[1]

    first, events, _ = gather_plan(1.0)
    number = {event[0]: k for k, event in enumerate(events)}

    def copy(key, off):
        part, axis, start, sign, hop = key
        half = hop == RINGS[axis] // 2
        groups = slice(0, SPLIT) if part == 0 else slice(SPLIT, 8)
        rows = slice(0, 32)
        if half:
            rows = slice(0, 16) if sign > 0 else slice(16, 32)
        k = number[key]
        chunk = member(off)
        step = [0, 0]
        step[axis] = sign
        own = off == (0, 0)
        src = own_ref.at[groups, rows] if own else out_ref.at[chunk, groups, rows]
        return pltpu.make_async_remote_copy(
            src_ref=src, dst_ref=out_ref.at[chunk, groups, rows], send_sem=send_sem.at[k], recv_sem=recv_sem.at[k],
            device_id={"chan": member(step)}, device_id_type=pl.DeviceIdType.MESH)

    barrier = pltpu.get_barrier_semaphore()
    for step in ((1, 0), (-1, 0), (0, 1), (0, -1)):
        pl.semaphore_signal(barrier, inc=1, device_id={"chan": member(step)},
                            device_id_type=pl.DeviceIdType.MESH)
    for k in range(1, slabs):
        pl.semaphore_signal(barrier, inc=1, device_id={"sky": lax.rem(sky + k, slabs)},
                            device_id_type=pl.DeviceIdType.MESH)
    pl.semaphore_wait(barrier, 3 + slabs)

    def exchange(k):
        to, source = lax.rem(sky + k, slabs), lax.rem(sky + slabs - k, slabs)
        out, landed = [pltpu.make_async_remote_copy(
            src_ref=amp_ref.at[to], dst_ref=own_ref.at[at], send_sem=sky_send_sem.at[k], recv_sem=sky_recv_sem.at[k],
            device_id={"sky": to}, device_id_type=pl.DeviceIdType.MESH) for at in (sky, source)]
        return out, landed

    swaps = [exchange(k) for k in range(1, slabs)]
    for out, _ in swaps:
        out.start()
    kept = pltpu.make_async_copy(amp_ref.at[sky], own_ref.at[sky], local_sem)
    kept.start()
    kept.wait()
    for _, landed in swaps:
        landed.wait_recv()
    sent = [copy(key, key[2]) for key in first]
    for c in sent:
        c.start()
    local = pltpu.make_async_copy(own_ref, out_ref.at[chan], local_sem)
    local.start()
    for key, moved, out in events:
        copy(key, moved).wait_recv()
        for nxt in out:
            c = copy(nxt, nxt[2])
            c.start()
            sent.append(c)
    local.wait()
    for c in sent:
        c.wait_send()
    for out, _ in swaps:
        out.wait_send()


def gather(amp):
    count = len(gather_plan(1.0)[1])
    return pl.pallas_call(
        gather_kernel,
        out_shape=jax.ShapeDtypeStruct((RINGS[0] * RINGS[1],) + amp.shape, jnp.float32),
        in_specs=[pl.BlockSpec(memory_space=pltpu.VMEM)],
        out_specs=pl.BlockSpec(memory_space=pltpu.VMEM),
        scratch_shapes=[pltpu.VMEM(amp.shape, jnp.float32), pltpu.SemaphoreType.DMA, pltpu.SemaphoreType.DMA((count,)),
                        pltpu.SemaphoreType.DMA((count,)), pltpu.SemaphoreType.DMA((8,)),
                        pltpu.SemaphoreType.DMA((8,))],
        compiler_params=pltpu.CompilerParams(collective_id=0, has_side_effects=True, vmem_limit_bytes=40 << 20),
    )(amp)


def clean_kernel(tmpl_ref, amp_ref, raw_ref, out_ref):
    owners = amp_ref.shape[0]
    for c in range(0, owners, 8):
        amp = jnp.concatenate([amp_ref[c + i, 0] for i in range(8)], axis=1)
        rest = raw_ref[0, :, c * BLK:(c + 8) * BLK] - mm_nn(tmpl_ref[...], amp)
        for i in range(8):
            out_ref[:, c + i, :] = rest[:, i * BLK:(i + 1) * BLK]


def clean(tmpl, amp, raw):
    owners, groups = amp.shape[0], amp.shape[1]
    rows = raw.shape[1]
    return pl.pallas_call(
        clean_kernel,
        grid=(groups,),
        out_shape=jax.ShapeDtypeStruct((rows, groups * owners, BLK), jnp.float32),
        in_specs=[pl.BlockSpec(tmpl.shape, lambda g: (0, 0)),
                  pl.BlockSpec((owners, 1, amp.shape[2], BLK), lambda g: (0, g, 0, 0)),
                  pl.BlockSpec((1, rows, owners * BLK), lambda g: (g, 0, 0))],
        out_specs=pl.BlockSpec((rows, owners, BLK), lambda g: (0, g, 0)),
    )(tmpl, amp, raw)


def tables(order_row, counts_row, dest_rows, slabs):
    slot_index = jnp.arange(CAP, dtype=jnp.int32)
    offsets = jnp.cumsum(counts_row) - counts_row
    live = slot_index[None, :] < counts_row[:, None]
    position = jnp.where(live, offsets[:, None] + slot_index[None, :], 0)
    slot_block = jnp.where(live, jnp.take(order_row, position, axis=0), -1)
    bound = dest_rows[None, :, :] == jnp.arange(slabs, dtype=jnp.int32)[:, None, None]
    slab_block = jnp.max(jnp.where(bound, slot_block[None, :, :], -1), axis=2)
    return slot_block.astype(jnp.int32), slab_block.astype(jnp.int32)


def on_device(sky_map, templates, noise_var, block_order, patch_count, slab_dest):
    slabs = lax.axis_size("sky")
    member = lax.axis_index("chan")
    rows = sky_map.shape[0]
    slot_block, slab_block = tables(block_order[0], patch_count[0], slab_dest[0], slabs)
    owners = slot_block.shape[0]
    outgoing = pack(slot_kernel, slot_block, (owners, rows, CAP * BLK), sky_map)
    sky_out = pack(slab_kernel, slab_block, (slabs, rows, owners * BLK), sky_map)
    pixels = lax.all_to_all(outgoing, "chan", split_axis=0, concat_axis=0, tiled=True)
    pixels = pixels.reshape(NU, CAP * BLK)
    pixels, sky_out = lax.optimization_barrier((pixels, sky_out))
    raw = lax.all_to_all(sky_out, "sky", split_axis=0, concat_axis=0, tiled=True)
    block_count = lax.dynamic_index_in_dim(patch_count[0], member, 0, keepdims=False)
    padded = jnp.pad(templates, ((0, 0), (0, 32 - templates.shape[1])))
    amp = gls(block_count.reshape(1, 1), pixels, padded.T, noise_var[None, :])
    amp, raw = lax.optimization_barrier((amp, raw))
    own_dest = lax.dynamic_index_in_dim(slab_dest[0], member, 0, keepdims=False)
    slot_index = jnp.arange(CAP, dtype=jnp.int32)
    match = (own_dest[None, :] == jnp.arange(slabs, dtype=jnp.int32)[:, None]) & (slot_index[None, :] < block_count)
    source = jnp.sum(jnp.where(match, slot_index[None, :], 0), axis=1)
    amp = jnp.take(amp.reshape(32, CAP, BLK).transpose(1, 0, 2), source, axis=0)
    amp = jnp.where(jnp.any(match, axis=1)[:, None, None], amp, 0.0)
    amp = gather(amp)
    own = lax.dynamic_slice_in_dim(padded, member * rows, rows, 0)
    return clean(own, amp, raw)


def solution(mesh):
    return jax.shard_map(
        on_device,
        mesh=mesh,
        in_specs=(P("chan", "sky"), P(), P(), P("sky", None), P("sky", None), P("sky", None, None)),
        out_specs=P("chan", "sky", None),
        check_vma=False,
    )
```

```python
import functools
import jax, jax.numpy as jnp
from jax import lax
from jax.sharding import PartitionSpec as P
from jax.experimental import pallas as pl
from jax.experimental.pallas import tpu as pltpu
NU = 1024
BLK = 128
CAP = 8
HI = lax.Precision.HIGHEST
NT_DIMS = (((1,), (1,)), ((), ()))
NN_DIMS = (((1,), (0,)), ((), ()))

def mm_nn(a, b):
    return lax.dot_general(a, b, NN_DIMS, precision=HI, preferred_element_type=jnp.float32)

def invert_spd(ref, slabs):
    lane = lax.broadcasted_iota(jnp.int32, (8, 128), 1)
    sub = lax.broadcasted_iota(jnp.int32, (8, 128), 0)
    for t in range(slabs):
        lo = 8 * t
        in_slab = (lane >= lo) & (lane < lo + 8)
        rows = [jnp.broadcast_to(ref[lo + i:lo + i + 1, :], (8, 128)) for i in range(8)]
        a = {}
        for i in range(8):
            for j in range(i + 1):
                a[i, j] = jnp.broadcast_to(rows[i][:, lo + j:lo + j + 1], (8, 128))
        low, inv = {}, []
        for j in range(8):
            r = 1.0 / a[j, j]
            inv.append(r)
            for i in range(j + 1, 8):
                low[i, j] = a[i, j] * r
            for i in range(j + 1, 8):
                for m in range(j + 1, i + 1):
                    a[i, m] = a[i, m] - low[i, j] * a[m, j]
        y = []
        for i in range(8):
            v = jnp.where(in_slab, jnp.where(lane == lo + i, 1.0, 0.0), rows[i])
            for j in range(i):
                v = v - low[i, j] * y[j]
            y.append(v)
        u = [None] * 8
        for i in reversed(range(8)):
            v = y[i] * inv[i]
            for j in range(7, i, -1):
                v = v - low[j, i] * u[j]
            u[i] = v
        for g in list(range(t + 1, slabs)) + list(range(t)):
            row = ref[8 * g:8 * g + 8, :]
            acc = jnp.where(in_slab, 0.0, row)
            for j in range(8):
                acc = acc - jnp.broadcast_to(row[:, lo + j:lo + j + 1], (8, 128)) * u[j]
            ref[8 * g:8 * g + 8, :] = acc
        own = u[0]
        for i in range(1, 8):
            own = jnp.where(sub == i, u[i], own)
        ref[lo:lo + 8, :] = own

def split3(a):
    hi = a.astype(jnp.bfloat16)
    rest = a - hi.astype(jnp.float32)
    mid = rest.astype(jnp.bfloat16)
    low = (rest - mid.astype(jnp.float32)).astype(jnp.bfloat16)
    return hi, mid, low

def cat(parts):
    return jnp.concatenate(parts, axis=1)

def dot6(a, b, dims):
    def one(x, y):
        return lax.dot_general(x, y, dims, preferred_element_type=jnp.float32)
    if dims is NT_DIMS:
        return one(cat(a[:1]), b[2]) + one(cat(a[:2]), cat([b[1]] * 2)) + one(cat(a), cat([b[0]] * 3))
    up = lambda y, k: jnp.concatenate([y] * k, axis=0)
    return one(cat(a[:1]), b[2]) + one(cat(a[:2]), up(b[1], 2)) + one(cat(a), up(b[0], 3))

def gls_kernel(cnt_ref, x_ref, tt_ref, noise_ref, out_ref, xs_ref, q_ref, v_ref, p_ref, d_ref, w_ref, m_ref, nb=8):
    scale = 1.0 / (cnt_ref[0, 0] * 128).astype(jnp.float32)
    n = 128 * nb
    ext = n + 32
    row = lax.broadcasted_iota(jnp.int32, (128, 128), 0)
    col = lax.broadcasted_iota(jnp.int32, (128, 128), 1)

    def split_rows(r, carry):
        at = pl.ds(pl.multiple_of(r * 128, 128), 128)
        for i, part in enumerate(split3(x_ref[at, :])):
            xs_ref[i, at, :] = part
        return carry
    lax.fori_loop(0, nb, split_rows, 0)

    def factor(k):
        lo, hi = 128 * k, 128 * k + 128
        value = dot6(split3(p_ref[hi:ext, :]), split3(d_ref[...]), NN_DIMS)
        for i, part in enumerate(split3(value)):
            v_ref[i, hi:ext, lo:hi] = part

    def step(k, carry):
        for kk in range(nb):
            @pl.when(k == kk)
            def _(kk=kk):
                lo, hi = 128 * kk, 128 * kk + 128
                if kk:
                    factor(kk - 1)
                p_ref[n:ext, :] = tt_ref[:, lo:hi]
                p_ref[lo:n, :] = dot6([xs_ref[i, lo:n, :] for i in range(3)],
                                      [xs_ref[i, lo:hi, :] for i in range(3)], NT_DIMS) * scale
                if kk:
                    p_ref[lo:ext, :] -= dot6([v_ref[i, lo:ext, 0:lo] for i in range(3)],
                                             [q_ref[i, lo:hi, 0:lo] for i in range(3)], NT_DIMS)
                if hi < n:
                    for i, part in enumerate(split3(p_ref[hi:n, :])):
                        q_ref[i, hi:n, lo:hi] = part
                noise = jnp.broadcast_to(noise_ref[0:1, lo:hi], (128, 128))
                d_ref[...] = p_ref[lo:hi, :] + jnp.where(row == col, noise, 0.0)
        invert_spd(d_ref, 16)
        return carry
    lax.fori_loop(0, nb, step, 0)
    factor(nb - 1)
    for k in reversed(range(nb)):
        lo, hi = 128 * k, 128 * k + 128
        wk = sum(v_ref[i, n:ext, lo:hi].astype(jnp.float32) for i in (2, 1, 0))
        if hi < n:
            wk = wk - dot6([w_ref[i, :, hi:n] for i in range(3)],
                           [v_ref[i, hi:n, lo:hi] for i in range(3)], NN_DIMS)
        for i, part in enumerate(split3(wk)):
            w_ref[i, :, lo:hi] = part
    w = [w_ref[i] for i in range(3)]
    proj = dot6(w, [xs_ref[i] for i in range(3)], NN_DIMS)
    gram = dot6(w, split3(tt_pad(tt_ref, n)), NT_DIMS)
    prow = lax.broadcasted_iota(jnp.int32, (32, 128), 0)
    pcol = lax.broadcasted_iota(jnp.int32, (32, 128), 1)
    m_ref[...] = gram + jnp.where((prow == pcol) & (prow >= 30), 1.0, 0.0)
    invert_spd(m_ref, 4)
    out_ref[...] = mm_nn(m_ref[...][:, 0:32], proj)

def tt_pad(tt_ref, n):
    return jnp.concatenate([tt_ref[...], jnp.zeros((96, n), jnp.float32)], axis=0)

def gls(cnt, x, tt, noise):
    n = x.shape[0]
    nb = n // 128
    return pl.pallas_call(
        functools.partial(gls_kernel, nb=nb),
        out_shape=jax.ShapeDtypeStruct((32, x.shape[1]), jnp.float32),
        in_specs=[pl.BlockSpec(memory_space=pltpu.SMEM)] + [pl.BlockSpec(memory_space=pltpu.VMEM)] * 3,
        out_specs=pl.BlockSpec(memory_space=pltpu.VMEM),
        scratch_shapes=[pltpu.VMEM((3, n, n), jnp.bfloat16), pltpu.VMEM((3, n, n), jnp.bfloat16),
                        pltpu.VMEM((3, n + 32, n), jnp.bfloat16), pltpu.VMEM((n + 32, 128), jnp.float32),
                        pltpu.VMEM((128, 128), jnp.float32), pltpu.VMEM((3, 32, n), jnp.bfloat16),
                        pltpu.VMEM((32, 128), jnp.float32)],
        cost_estimate=pl.CostEstimate(flops=60 * 10**9, bytes_accessed=1 << 22, transcendentals=0),
        compiler_params=pltpu.CompilerParams(vmem_limit_bytes=40 << 20),
    )(cnt, x, tt, noise)


def slot_kernel(slot_ref, map_ref, out_ref):
    def put(c, carry):
        for j in range(CAP):
            block = slot_ref[c, j]
            at = pl.multiple_of(jnp.maximum(block, 0) * BLK, BLK)
            tile = map_ref[:, pl.ds(at, BLK)]
            out_ref[c, :, j * BLK:(j + 1) * BLK] = jnp.where(block >= 0, tile, 0.0)
        return carry
    lax.fori_loop(0, slot_ref.shape[0], put, 0)


def slab_kernel(slab_ref, map_ref, out_ref):
    def put(c, carry):
        place = pl.multiple_of(c * BLK, BLK)
        for d in range(out_ref.shape[0]):
            block = slab_ref[d, c]
            at = pl.multiple_of(jnp.maximum(block, 0) * BLK, BLK)
            tile = map_ref[:, pl.ds(at, BLK)]
            out_ref[d, :, pl.ds(place, BLK)] = jnp.where(block >= 0, tile, 0.0)
        return carry
    lax.fori_loop(0, slab_ref.shape[1], put, 0)


def pack(kernel, blocks, shape, sky_map):
    return pl.pallas_call(
        kernel,
        out_shape=jax.ShapeDtypeStruct(shape, jnp.float32),
        in_specs=[pl.BlockSpec(memory_space=pltpu.SMEM), pl.BlockSpec(memory_space=pltpu.VMEM)],
        out_specs=pl.BlockSpec(memory_space=pltpu.VMEM),
        cost_estimate=pl.CostEstimate(flops=10**6, bytes_accessed=6 << 20, transcendentals=0),
        compiler_params=pltpu.CompilerParams(vmem_limit_bytes=40 << 20),
    )(blocks, sky_map)


RINGS = (8, 4)
SPLIT = 5


def gather_plan(cost):
    time, free, queue, serial = 0.0, {}, [], 0
    events = []

    def send(now, part, axis, off, sign, hop):
        nonlocal serial
        half = hop == RINGS[axis] // 2
        groups = SPLIT if part == 0 else 8 - SPLIT
        link = (axis, sign)
        start = max(now, free.get(link, 0.0))
        free[link] = start + cost * groups * (0.5 if half else 1.0)
        serial += 1
        queue.append((free[link] + 2.0, serial, (part, axis, off, sign, hop)))
        return part, axis, off, sign, hop

    def both(now, part, axis, off):
        return [send(now, part, axis, off, sign, 1) for sign in (1, -1)]

    first = []
    for part in (0, 1):
        first += both(0.0, part, part, (0, 0))
    for part in (0, 1):
        first += both(0.0, part, 1 - part, (0, 0))
    halves = set()
    while queue:
        queue.sort()
        time, _, (part, axis, off, sign, hop) = queue.pop(0)
        moved = list(off)
        moved[axis] -= sign
        moved = tuple(moved)
        half = hop == RINGS[axis] // 2
        out = []
        if not half:
            out.append(send(time, part, axis, moved, sign, hop + 1))
        if axis == part:
            place = (part, moved[axis] % RINGS[axis])
            if not half or place in halves:
                out += both(time, part, 1 - axis, moved)
            halves.add(place)
        events.append(((part, axis, off, sign, hop), moved, out))
    return first, events, time


def gather_kernel(amp_ref, tmpl_ref, raw_ref, out_ref, all_ref, own_ref, pix_ref, local_sem, pix_sem, send_sem, recv_sem,
                  sky_send_sem, sky_recv_sem):
    pixels = pltpu.make_async_copy(raw_ref, pix_ref, pix_sem)
    pixels.start()
    chan = lax.axis_index("chan")
    sky = lax.axis_index("sky")
    slabs = amp_ref.shape[0]
    place = (chan // RINGS[1], lax.rem(chan, RINGS[1]))

    def member(off):
        at = [lax.rem(place[i] + off[i] % RINGS[i], RINGS[i]) for i in (0, 1)]
        return at[0] * RINGS[1] + at[1]

    first, events, _ = gather_plan(1.0)
    number = {event[0]: k for k, event in enumerate(events)}

    def copy(key, off):
        part, axis, start, sign, hop = key
        half = hop == RINGS[axis] // 2
        groups = slice(0, SPLIT) if part == 0 else slice(SPLIT, 8)
        rows = slice(0, 32)
        if half:
            rows = slice(0, 16) if sign > 0 else slice(16, 32)
        k = number[key]
        chunk = member(off)
        step = [0, 0]
        step[axis] = sign
        own = off == (0, 0)
        src = own_ref.at[groups, rows] if own else all_ref.at[chunk, groups, rows]
        return pltpu.make_async_remote_copy(
            src_ref=src, dst_ref=all_ref.at[chunk, groups, rows], send_sem=send_sem.at[k], recv_sem=recv_sem.at[k],
            device_id={"chan": member(step)}, device_id_type=pl.DeviceIdType.MESH)

    barrier = pltpu.get_barrier_semaphore()
    for step in ((1, 0), (-1, 0), (0, 1), (0, -1)):
        pl.semaphore_signal(barrier, inc=1, device_id={"chan": member(step)},
                            device_id_type=pl.DeviceIdType.MESH)
    for k in range(1, slabs):
        pl.semaphore_signal(barrier, inc=1, device_id={"sky": lax.rem(sky + k, slabs)},
                            device_id_type=pl.DeviceIdType.MESH)
    pl.semaphore_wait(barrier, 3 + slabs)

    def exchange(k):
        to, source = lax.rem(sky + k, slabs), lax.rem(sky + slabs - k, slabs)
        out, landed = [pltpu.make_async_remote_copy(
            src_ref=amp_ref.at[to], dst_ref=own_ref.at[at], send_sem=sky_send_sem.at[k], recv_sem=sky_recv_sem.at[k],
            device_id={"sky": to}, device_id_type=pl.DeviceIdType.MESH) for at in (sky, source)]
        return out, landed

    swaps = [exchange(k) for k in range(1, slabs)]
    for out, _ in swaps:
        out.start()
    kept = pltpu.make_async_copy(amp_ref.at[sky], own_ref.at[sky], local_sem)
    kept.start()
    kept.wait()
    for _, landed in swaps:
        landed.wait_recv()
    sent = [copy(key, key[2]) for key in first]
    for c in sent:
        c.start()
    hi, mid, low = split3(tmpl_ref[...])
    tmpl = cat([hi, hi, mid, hi, mid, low])

    def clean(part, off):
        chunk = member(off)
        groups = range(0, SPLIT) if part == 0 else range(SPLIT, 8)
        amp = cat([own_ref[g] if off == (0, 0) else all_ref[chunk, g] for g in groups])
        hi, mid, low = split3(amp)
        model = lax.dot_general(tmpl, jnp.concatenate([low, mid, mid, hi, hi, hi], axis=0), NN_DIMS,
                                preferred_element_type=jnp.float32)
        at = pl.ds(pl.multiple_of(chunk * BLK, BLK), BLK)
        for i, g in enumerate(groups):
            rest = pix_ref[g, :, at] - model[:, i * BLK:(i + 1) * BLK]
            out_ref[:, pl.ds(g * (RINGS[0] * RINGS[1]) + chunk, 1), :] = rest[:, None, :]

    pixels.wait()
    for part in (0, 1):
        clean(part, (0, 0))
    halves = set()
    for key, moved, out in events:
        copy(key, moved).wait_recv()
        for nxt in out:
            c = copy(nxt, nxt[2])
            c.start()
            sent.append(c)
        part, axis, _, _, hop = key
        where = (part, moved[0] % RINGS[0], moved[1] % RINGS[1])
        if hop < RINGS[axis] // 2 or where in halves:
            clean(part, moved)
        halves.add(where)
    for c in sent:
        c.wait_send()
    for out, _ in swaps:
        out.wait_send()


def gather_clean(amp, tmpl, raw):
    count = len(gather_plan(1.0)[1])
    owners, groups = RINGS[0] * RINGS[1], amp.shape[0]
    return pl.pallas_call(
        gather_kernel,
        out_shape=jax.ShapeDtypeStruct((tmpl.shape[0], groups * owners, BLK), jnp.float32),
        in_specs=[pl.BlockSpec(memory_space=pltpu.VMEM)] * 2 + [pl.BlockSpec(memory_space=pl.ANY)],
        out_specs=pl.BlockSpec(memory_space=pltpu.VMEM),
        scratch_shapes=[pltpu.VMEM((owners,) + amp.shape, jnp.float32), pltpu.VMEM(amp.shape, jnp.float32),
                        pltpu.VMEM(raw.shape, jnp.float32), pltpu.SemaphoreType.DMA, pltpu.SemaphoreType.DMA,
                        pltpu.SemaphoreType.DMA((count,)), pltpu.SemaphoreType.DMA((count,)),
                        pltpu.SemaphoreType.DMA((8,)), pltpu.SemaphoreType.DMA((8,))],
        compiler_params=pltpu.CompilerParams(collective_id=0, has_side_effects=True, vmem_limit_bytes=40 << 20),
    )(amp, tmpl, raw)


def tables(order_row, counts_row, dest_rows, slabs):
    slot_index = jnp.arange(CAP, dtype=jnp.int32)
    offsets = jnp.cumsum(counts_row) - counts_row
    live = slot_index[None, :] < counts_row[:, None]
    position = jnp.where(live, offsets[:, None] + slot_index[None, :], 0)
    slot_block = jnp.where(live, jnp.take(order_row, position, axis=0), -1)
    bound = dest_rows[None, :, :] == jnp.arange(slabs, dtype=jnp.int32)[:, None, None]
    slab_block = jnp.max(jnp.where(bound, slot_block[None, :, :], -1), axis=2)
    return slot_block.astype(jnp.int32), slab_block.astype(jnp.int32)


def on_device(sky_map, templates, noise_var, block_order, patch_count, slab_dest):
    slabs = lax.axis_size("sky")
    member = lax.axis_index("chan")
    rows = sky_map.shape[0]
    slot_block, slab_block = tables(block_order[0], patch_count[0], slab_dest[0], slabs)
    owners = slot_block.shape[0]
    outgoing = pack(slot_kernel, slot_block, (owners, rows, CAP * BLK), sky_map)
    sky_out = pack(slab_kernel, slab_block, (slabs, rows, owners * BLK), sky_map)
    pixels = lax.all_to_all(outgoing, "chan", split_axis=0, concat_axis=0, tiled=True)
    pixels = pixels.reshape(NU, CAP * BLK)
    pixels, sky_out = lax.optimization_barrier((pixels, sky_out))
    raw = lax.all_to_all(sky_out, "sky", split_axis=0, concat_axis=0, tiled=True)
    block_count = lax.dynamic_index_in_dim(patch_count[0], member, 0, keepdims=False)
    padded = jnp.pad(templates, ((0, 0), (0, 32 - templates.shape[1])))
    amp = gls(block_count.reshape(1, 1), pixels, padded.T, noise_var[None, :])
    amp, raw = lax.optimization_barrier((amp, raw))
    own_dest = lax.dynamic_index_in_dim(slab_dest[0], member, 0, keepdims=False)
    slot_index = jnp.arange(CAP, dtype=jnp.int32)
    match = (own_dest[None, :] == jnp.arange(slabs, dtype=jnp.int32)[:, None]) & (slot_index[None, :] < block_count)
    source = jnp.sum(jnp.where(match, slot_index[None, :], 0), axis=1)
    amp = jnp.take(amp.reshape(32, CAP, BLK).transpose(1, 0, 2), source, axis=0)
    amp = jnp.where(jnp.any(match, axis=1)[:, None, None], amp, 0.0)
    own = lax.dynamic_slice_in_dim(padded, member * rows, rows, 0)
    return gather_clean(amp, own, raw)


def solution(mesh):
    return jax.shard_map(
        on_device,
        mesh=mesh,
        in_specs=(P("chan", "sky"), P(), P(), P("sky", None), P("sky", None), P("sky", None, None)),
        out_specs=P("chan", "sky", None),
        check_vma=False,
    )
```

```python
import functools
import jax, jax.numpy as jnp
from jax import lax
from jax.sharding import PartitionSpec as P
from jax.experimental import pallas as pl
from jax.experimental.pallas import tpu as pltpu
NU = 1024
BLK = 128
CAP = 8
HI = lax.Precision.HIGHEST
NT_DIMS = (((1,), (1,)), ((), ()))
NN_DIMS = (((1,), (0,)), ((), ()))

def mm_nn(a, b):
    return lax.dot_general(a, b, NN_DIMS, precision=HI, preferred_element_type=jnp.float32)

def invert_spd(ref, slabs):
    lane = lax.broadcasted_iota(jnp.int32, (8, 128), 1)
    sub = lax.broadcasted_iota(jnp.int32, (8, 128), 0)
    for t in range(slabs):
        lo = 8 * t
        in_slab = (lane >= lo) & (lane < lo + 8)
        rows = [jnp.broadcast_to(ref[lo + i:lo + i + 1, :], (8, 128)) for i in range(8)]
        a = {}
        for i in range(8):
            for j in range(i + 1):
                a[i, j] = jnp.broadcast_to(rows[i][:, lo + j:lo + j + 1], (8, 128))
        low, inv = {}, []
        for j in range(8):
            r = 1.0 / a[j, j]
            inv.append(r)
            for i in range(j + 1, 8):
                low[i, j] = a[i, j] * r
            for i in range(j + 1, 8):
                for m in range(j + 1, i + 1):
                    a[i, m] = a[i, m] - low[i, j] * a[m, j]
        y = []
        for i in range(8):
            v = jnp.where(in_slab, jnp.where(lane == lo + i, 1.0, 0.0), rows[i])
            for j in range(i):
                v = v - low[i, j] * y[j]
            y.append(v)
        u = [None] * 8
        for i in reversed(range(8)):
            v = y[i] * inv[i]
            for j in range(7, i, -1):
                v = v - low[j, i] * u[j]
            u[i] = v
        for g in list(range(t + 1, slabs)) + list(range(t)):
            row = ref[8 * g:8 * g + 8, :]
            acc = jnp.where(in_slab, 0.0, row)
            for j in range(8):
                acc = acc - jnp.broadcast_to(row[:, lo + j:lo + j + 1], (8, 128)) * u[j]
            ref[8 * g:8 * g + 8, :] = acc
        own = u[0]
        for i in range(1, 8):
            own = jnp.where(sub == i, u[i], own)
        ref[lo:lo + 8, :] = own

def split3(a):
    hi = a.astype(jnp.bfloat16)
    rest = a - hi.astype(jnp.float32)
    mid = rest.astype(jnp.bfloat16)
    low = (rest - mid.astype(jnp.float32)).astype(jnp.bfloat16)
    return hi, mid, low

def cat(parts):
    return jnp.concatenate(parts, axis=1)

def dot6(a, b, dims):
    def one(x, y):
        return lax.dot_general(x, y, dims, preferred_element_type=jnp.float32)
    if dims is NT_DIMS:
        return one(cat(a[:1]), b[2]) + one(cat(a[:2]), cat([b[1]] * 2)) + one(cat(a), cat([b[0]] * 3))
    up = lambda y, k: jnp.concatenate([y] * k, axis=0)
    return one(cat(a[:1]), b[2]) + one(cat(a[:2]), up(b[1], 2)) + one(cat(a), up(b[0], 3))

def gls_kernel(cnt_ref, x_ref, tt_ref, noise_ref, out_ref, xs_ref, q_ref, v_ref, p_ref, d_ref, w_ref, m_ref, nb=8):
    scale = 1.0 / (cnt_ref[0, 0] * 128).astype(jnp.float32)
    n = 128 * nb
    ext = n + 32
    row = lax.broadcasted_iota(jnp.int32, (128, 128), 0)
    col = lax.broadcasted_iota(jnp.int32, (128, 128), 1)

    def split_rows(r, carry):
        at = pl.ds(pl.multiple_of(r * 128, 128), 128)
        for i, part in enumerate(split3(x_ref[at, :])):
            xs_ref[i, at, :] = part
        return carry
    lax.fori_loop(0, nb, split_rows, 0)

    def factor(k):
        lo, hi = 128 * k, 128 * k + 128
        value = dot6(split3(p_ref[hi:ext, :]), split3(d_ref[...]), NN_DIMS)
        for i, part in enumerate(split3(value)):
            v_ref[i, hi:ext, lo:hi] = part

    def step(k, carry):
        for kk in range(nb):
            @pl.when(k == kk)
            def _(kk=kk):
                lo, hi = 128 * kk, 128 * kk + 128
                if kk:
                    factor(kk - 1)
                p_ref[n:ext, :] = tt_ref[:, lo:hi]
                p_ref[lo:n, :] = dot6([xs_ref[i, lo:n, :] for i in range(3)],
                                      [xs_ref[i, lo:hi, :] for i in range(3)], NT_DIMS) * scale
                if kk:
                    p_ref[lo:ext, :] -= dot6([v_ref[i, lo:ext, 0:lo] for i in range(3)],
                                             [q_ref[i, lo:hi, 0:lo] for i in range(3)], NT_DIMS)
                if hi < n:
                    for i, part in enumerate(split3(p_ref[hi:n, :])):
                        q_ref[i, hi:n, lo:hi] = part
                noise = jnp.broadcast_to(noise_ref[0:1, lo:hi], (128, 128))
                d_ref[...] = p_ref[lo:hi, :] + jnp.where(row == col, noise, 0.0)
        invert_spd(d_ref, 16)
        return carry
    lax.fori_loop(0, nb, step, 0)
    factor(nb - 1)
    for k in reversed(range(nb)):
        lo, hi = 128 * k, 128 * k + 128
        wk = sum(v_ref[i, n:ext, lo:hi].astype(jnp.float32) for i in (2, 1, 0))
        if hi < n:
            wk = wk - dot6([w_ref[i, :, hi:n] for i in range(3)],
                           [v_ref[i, hi:n, lo:hi] for i in range(3)], NN_DIMS)
        for i, part in enumerate(split3(wk)):
            w_ref[i, :, lo:hi] = part
    w = [w_ref[i] for i in range(3)]
    proj = dot6(w, [xs_ref[i] for i in range(3)], NN_DIMS)
    gram = dot6(w, split3(tt_pad(tt_ref, n)), NT_DIMS)
    prow = lax.broadcasted_iota(jnp.int32, (32, 128), 0)
    pcol = lax.broadcasted_iota(jnp.int32, (32, 128), 1)
    m_ref[...] = gram + jnp.where((prow == pcol) & (prow >= 30), 1.0, 0.0)
    invert_spd(m_ref, 4)
    out_ref[...] = mm_nn(m_ref[...][:, 0:32], proj)

def tt_pad(tt_ref, n):
    return jnp.concatenate([tt_ref[...], jnp.zeros((96, n), jnp.float32)], axis=0)

def gls(cnt, x, tt, noise):
    n = x.shape[0]
    nb = n // 128
    return pl.pallas_call(
        functools.partial(gls_kernel, nb=nb),
        out_shape=jax.ShapeDtypeStruct((32, x.shape[1]), jnp.float32),
        in_specs=[pl.BlockSpec(memory_space=pltpu.SMEM)] + [pl.BlockSpec(memory_space=pltpu.VMEM)] * 3,
        out_specs=pl.BlockSpec(memory_space=pltpu.VMEM),
        scratch_shapes=[pltpu.VMEM((3, n, n), jnp.bfloat16), pltpu.VMEM((3, n, n), jnp.bfloat16),
                        pltpu.VMEM((3, n + 32, n), jnp.bfloat16), pltpu.VMEM((n + 32, 128), jnp.float32),
                        pltpu.VMEM((128, 128), jnp.float32), pltpu.VMEM((3, 32, n), jnp.bfloat16),
                        pltpu.VMEM((32, 128), jnp.float32)],
        cost_estimate=pl.CostEstimate(flops=60 * 10**9, bytes_accessed=1 << 22, transcendentals=0),
        compiler_params=pltpu.CompilerParams(vmem_limit_bytes=40 << 20),
    )(cnt, x, tt, noise)


def slot_kernel(slot_ref, map_ref, out_ref):
    owners = out_ref.shape[0]
    base = pl.program_id(0) * owners

    def put(c, carry):
        for j in range(CAP):
            block = slot_ref[base + c, j]
            at = pl.multiple_of(jnp.maximum(block, 0) * BLK, BLK)
            tile = map_ref[:, pl.ds(at, BLK)]
            out_ref[c, :, j * BLK:(j + 1) * BLK] = jnp.where(block >= 0, tile, 0.0)
        return carry
    lax.fori_loop(0, owners, put, 0)


def slab_kernel(slab_ref, map_ref, out_ref):
    def put(c, carry):
        place = pl.multiple_of(c * BLK, BLK)
        for d in range(out_ref.shape[0]):
            block = slab_ref[d, c]
            at = pl.multiple_of(jnp.maximum(block, 0) * BLK, BLK)
            tile = map_ref[:, pl.ds(at, BLK)]
            out_ref[d, :, pl.ds(place, BLK)] = jnp.where(block >= 0, tile, 0.0)
        return carry
    lax.fori_loop(0, slab_ref.shape[1], put, 0)


def pack(kernel, blocks, shape, sky_map, steps=1):
    return pl.pallas_call(
        kernel,
        grid=(steps,),
        out_shape=pltpu.MemorySpace.HBM(shape, jnp.float32),
        in_specs=[pl.BlockSpec(memory_space=pltpu.SMEM), pl.BlockSpec(memory_space=pltpu.VMEM)],
        out_specs=pl.BlockSpec((shape[0] // steps,) + shape[1:], lambda g: (g, 0, 0)),
        cost_estimate=pl.CostEstimate(flops=10**6, bytes_accessed=6 << 20, transcendentals=0),
        compiler_params=pltpu.CompilerParams(vmem_limit_bytes=40 << 20),
    )(blocks, sky_map)


RINGS = (8, 4)
SPLIT = 5


def gather_plan(cost):
    time, free, queue, serial = 0.0, {}, [], 0
    events = []

    def send(now, part, axis, off, sign, hop):
        nonlocal serial
        half = hop == RINGS[axis] // 2
        groups = SPLIT if part == 0 else 8 - SPLIT
        link = (axis, sign)
        start = max(now, free.get(link, 0.0))
        free[link] = start + cost * groups * (0.5 if half else 1.0)
        serial += 1
        queue.append((free[link] + 2.0, serial, (part, axis, off, sign, hop)))
        return part, axis, off, sign, hop

    def both(now, part, axis, off):
        return [send(now, part, axis, off, sign, 1) for sign in (1, -1)]

    first = []
    for part in (0, 1):
        first += both(0.0, part, part, (0, 0))
    for part in (0, 1):
        first += both(0.0, part, 1 - part, (0, 0))
    halves = set()
    while queue:
        queue.sort()
        time, _, (part, axis, off, sign, hop) = queue.pop(0)
        moved = list(off)
        moved[axis] -= sign
        moved = tuple(moved)
        half = hop == RINGS[axis] // 2
        out = []
        if not half:
            out.append(send(time, part, axis, moved, sign, hop + 1))
        if axis == part:
            place = (part, moved[axis] % RINGS[axis])
            if not half or place in halves:
                out += both(time, part, 1 - axis, moved)
            halves.add(place)
        events.append(((part, axis, off, sign, hop), moved, out))
    return first, events, time


def gather_kernel(amp_ref, tmpl_ref, raw_ref, out_ref, all_ref, own_ref, pix_ref, local_sem, pix_sem, send_sem, recv_sem,
                  sky_send_sem, sky_recv_sem):
    pixels = pltpu.make_async_copy(raw_ref, pix_ref, pix_sem)
    pixels.start()
    chan = lax.axis_index("chan")
    sky = lax.axis_index("sky")
    slabs = amp_ref.shape[0]
    place = (chan // RINGS[1], lax.rem(chan, RINGS[1]))

    def member(off):
        at = [lax.rem(place[i] + off[i] % RINGS[i], RINGS[i]) for i in (0, 1)]
        return at[0] * RINGS[1] + at[1]

    first, events, _ = gather_plan(1.0)
    number = {event[0]: k for k, event in enumerate(events)}

    def copy(key, off):
        part, axis, start, sign, hop = key
        half = hop == RINGS[axis] // 2
        groups = slice(0, SPLIT) if part == 0 else slice(SPLIT, 8)
        rows = slice(0, 32)
        if half:
            rows = slice(0, 16) if sign > 0 else slice(16, 32)
        k = number[key]
        chunk = member(off)
        step = [0, 0]
        step[axis] = sign
        own = off == (0, 0)
        src = own_ref.at[groups, rows] if own else all_ref.at[chunk, groups, rows]
        return pltpu.make_async_remote_copy(
            src_ref=src, dst_ref=all_ref.at[chunk, groups, rows], send_sem=send_sem.at[k], recv_sem=recv_sem.at[k],
            device_id={"chan": member(step)}, device_id_type=pl.DeviceIdType.MESH)

    barrier = pltpu.get_barrier_semaphore()
    for step in ((1, 0), (-1, 0), (0, 1), (0, -1)):
        pl.semaphore_signal(barrier, inc=1, device_id={"chan": member(step)},
                            device_id_type=pl.DeviceIdType.MESH)
    for k in range(1, slabs):
        pl.semaphore_signal(barrier, inc=1, device_id={"sky": lax.rem(sky + k, slabs)},
                            device_id_type=pl.DeviceIdType.MESH)
    pl.semaphore_wait(barrier, 3 + slabs)

    def exchange(k):
        to, source = lax.rem(sky + k, slabs), lax.rem(sky + slabs - k, slabs)
        out, landed = [pltpu.make_async_remote_copy(
            src_ref=amp_ref.at[to], dst_ref=own_ref.at[at], send_sem=sky_send_sem.at[k], recv_sem=sky_recv_sem.at[k],
            device_id={"sky": to}, device_id_type=pl.DeviceIdType.MESH) for at in (sky, source)]
        return out, landed

    swaps = [exchange(k) for k in range(1, slabs)]
    for out, _ in swaps:
        out.start()
    kept = pltpu.make_async_copy(amp_ref.at[sky], own_ref.at[sky], local_sem)
    kept.start()
    kept.wait()
    for _, landed in swaps:
        landed.wait_recv()
    sent = [copy(key, key[2]) for key in first]
    for c in sent:
        c.start()
    hi, mid, low = split3(tmpl_ref[...])
    tmpl = cat([hi, hi, mid, hi, mid, low])

    def clean(part, off):
        chunk = member(off)
        groups = range(0, SPLIT) if part == 0 else range(SPLIT, 8)
        amp = cat([own_ref[g] if off == (0, 0) else all_ref[chunk, g] for g in groups])
        hi, mid, low = split3(amp)
        model = lax.dot_general(tmpl, jnp.concatenate([low, mid, mid, hi, hi, hi], axis=0), NN_DIMS,
                                preferred_element_type=jnp.float32)
        at = pl.ds(pl.multiple_of(chunk * BLK, BLK), BLK)
        for i, g in enumerate(groups):
            rest = pix_ref[g, :, at] - model[:, i * BLK:(i + 1) * BLK]
            out_ref[:, pl.ds(g * (RINGS[0] * RINGS[1]) + chunk, 1), :] = rest[:, None, :]

    pixels.wait()
    for part in (0, 1):
        clean(part, (0, 0))
    halves = set()
    for key, moved, out in events:
        copy(key, moved).wait_recv()
        for nxt in out:
            c = copy(nxt, nxt[2])
            c.start()
            sent.append(c)
        part, axis, _, _, hop = key
        where = (part, moved[0] % RINGS[0], moved[1] % RINGS[1])
        if hop < RINGS[axis] // 2 or where in halves:
            clean(part, moved)
        halves.add(where)
    for c in sent:
        c.wait_send()
    for out, _ in swaps:
        out.wait_send()


def gather_clean(amp, tmpl, raw):
    count = len(gather_plan(1.0)[1])
    owners, groups = RINGS[0] * RINGS[1], amp.shape[0]
    return pl.pallas_call(
        gather_kernel,
        out_shape=jax.ShapeDtypeStruct((tmpl.shape[0], groups * owners, BLK), jnp.float32),
        in_specs=[pl.BlockSpec(memory_space=pltpu.VMEM)] * 2 + [pl.BlockSpec(memory_space=pl.ANY)],
        out_specs=pl.BlockSpec(memory_space=pltpu.VMEM),
        scratch_shapes=[pltpu.VMEM((owners,) + amp.shape, jnp.float32), pltpu.VMEM(amp.shape, jnp.float32),
                        pltpu.VMEM(raw.shape, jnp.float32), pltpu.SemaphoreType.DMA, pltpu.SemaphoreType.DMA,
                        pltpu.SemaphoreType.DMA((count,)), pltpu.SemaphoreType.DMA((count,)),
                        pltpu.SemaphoreType.DMA((8,)), pltpu.SemaphoreType.DMA((8,))],
        compiler_params=pltpu.CompilerParams(collective_id=0, has_side_effects=True, vmem_limit_bytes=40 << 20),
    )(amp, tmpl, raw)


def tables(order_row, counts_row, dest_rows, slabs):
    slot_index = jnp.arange(CAP, dtype=jnp.int32)
    offsets = jnp.cumsum(counts_row) - counts_row
    live = slot_index[None, :] < counts_row[:, None]
    position = jnp.where(live, offsets[:, None] + slot_index[None, :], 0)
    slot_block = jnp.where(live, jnp.take(order_row, position, axis=0), -1)
    bound = dest_rows[None, :, :] == jnp.arange(slabs, dtype=jnp.int32)[:, None, None]
    slab_block = jnp.max(jnp.where(bound, slot_block[None, :, :], -1), axis=2)
    return slot_block.astype(jnp.int32), slab_block.astype(jnp.int32)


def on_device(sky_map, templates, noise_var, block_order, patch_count, slab_dest):
    slabs = lax.axis_size("sky")
    member = lax.axis_index("chan")
    rows = sky_map.shape[0]
    slot_block, slab_block = tables(block_order[0], patch_count[0], slab_dest[0], slabs)
    owners = slot_block.shape[0]
    outgoing = pack(slot_kernel, slot_block, (owners, rows, CAP * BLK), sky_map, steps=8)
    sky_out = pack(slab_kernel, slab_block, (slabs, rows, owners * BLK), sky_map)
    pixels = lax.all_to_all(outgoing, "chan", split_axis=0, concat_axis=0, tiled=True)
    pixels = pixels.reshape(NU, CAP * BLK)
    pixels, sky_out = lax.optimization_barrier((pixels, sky_out))
    raw = lax.all_to_all(sky_out, "sky", split_axis=0, concat_axis=0, tiled=True)
    block_count = lax.dynamic_index_in_dim(patch_count[0], member, 0, keepdims=False)
    padded = jnp.pad(templates, ((0, 0), (0, 32 - templates.shape[1])))
    amp = gls(block_count.reshape(1, 1), pixels, padded.T, noise_var[None, :])
    amp, raw = lax.optimization_barrier((amp, raw))
    own_dest = lax.dynamic_index_in_dim(slab_dest[0], member, 0, keepdims=False)
    slot_index = jnp.arange(CAP, dtype=jnp.int32)
    match = (own_dest[None, :] == jnp.arange(slabs, dtype=jnp.int32)[:, None]) & (slot_index[None, :] < block_count)
    source = jnp.sum(jnp.where(match, slot_index[None, :], 0), axis=1)
    amp = jnp.take(amp.reshape(32, CAP, BLK).transpose(1, 0, 2), source, axis=0)
    amp = jnp.where(jnp.any(match, axis=1)[:, None, None], amp, 0.0)
    own = lax.dynamic_slice_in_dim(padded, member * rows, rows, 0)
    return gather_clean(amp, own, raw)


def solution(mesh):
    return jax.shard_map(
        on_device,
        mesh=mesh,
        in_specs=(P("chan", "sky"), P(), P(), P("sky", None), P("sky", None), P("sky", None, None)),
        out_specs=P("chan", "sky", None),
        check_vma=False,
    )
```
